32 devices in a mesh: dp: 8 (over z, x), tensor: 4 (over y, core).
Axes of the slice: x: 2, y: 2, z: 4, core: 2. Of those that a mesh axis runs over, the one named last changes fastest.
Arguments:
- hidden: bfloat16 [8192, 1024], P('dp'), may hold values from -6 to 6
- cotangent: bfloat16 [8192, 1024], P('dp'), may hold values from -6 to 6
- norm_gain: float32 [1024], replicated, may hold values from 0.5 to 1.5
- gate_weight: bfloat16 [1024, 2048], P(None, 'tensor'), may hold values from -0.1875 to 0.1875
- value_weight: bfloat16 [1024, 2048], P(None, 'tensor'), may hold values from -0.1875 to 0.1875
- step_weight: bfloat16 [1024, 32], P(None, 'tensor'), may hold values from -0.1875 to 0.1875
- state_weight: bfloat16 [1024, 256], replicated, may hold values from -0.1875 to 0.1875
- value_kernel: float32 [4, 2048], P(None, 'tensor'), may hold values from -3 to 3
- value_offset: float32 [2048], P('tensor'), may hold values from -3 to 3
- state_kernel: float32 [4, 256], replicated, may hold values from -3 to 3
- state_offset: float32 [256], replicated, may hold values from -3 to 3
- step_offset: float32 [32], P('tensor'), may hold values from -6.5 to -2.5
- log_decay: float32 [32], P('tensor'), may hold values from 0 to 2.8
- skip_gain: float32 [32], P('tensor'), may hold values from 0.5 to 1.5
- mixer_gain: float32 [2048], P('tensor'), may hold values from 0.5 to 1.5
- output_weight: bfloat16 [2048, 1024], P('tensor'), may hold values from -0.125 to 0.125
Outputs:
- output: bfloat16 [8192, 1024], P('dp')
- hidden_gradient: float32 [8192, 1024], P('dp')
- gain_gradient: float32 [1024], replicated
- gate_gradient: float32 [1024, 2048], P(None, 'tensor')
- value_gradient: float32 [1024, 2048], P(None, 'tensor')
- step_gradient: float32 [1024, 32], P(None, 'tensor')
- state_gradient: float32 [1024, 256], replicated
- kernel_gradient: float32 [4, 2048], P(None, 'tensor')
- offset_gradient: float32 [2048], P('tensor')
- filter_gradient: float32 [4, 256], replicated
- shift_gradient: float32 [256], replicated
- timing_gradient: float32 [32], P('tensor')
- decay_gradient: float32 [32], P('tensor')
- skip_gradient: float32 [32], P('tensor')
- mixing_gradient: float32 [2048], P('tensor')
- output_gradient: float32 [2048, 1024], P('tensor')
The draws below stay inside these ranges and needn't reach their ends.
All inputs are finite; a program needn't handle non-finite values.
Results may differ from the reference program's by a relative error of at most 0.012.
Values sent between devices are 32-bit elements; how exact they have to be, the bound alone decides.
No kernel may reach another device: no remote copies, remote signals or barrier semaphores. Data moves between devices by JAX's collectives and lax.ppermute only.
A program may use at most 128 MiB of HBM per device.

```python
import jax
import jax.numpy as jnp
from jax import lax

D = 1024
HEADS = 32
STATE = 128
CONV = 4
GROUP = 256
SEQ_LEN = 1024
INNER = 2048
TOKENS = 8192


def block_levels(rng, shape, shards, low, high):
    def one(dim, blocks):
        heights = jax.random.uniform(jax.random.fold_in(jax.random.fold_in(rng, 6), dim), (blocks,), jnp.float32, low / len(shards), high / len(shards))
        return jnp.repeat(jnp.exp(heights), shape[dim] // blocks).reshape((-1,) + (1,) * (len(shape) - dim - 1))

    factor_of = one(*shards[0])
    for cut in shards[1:]:
        factor_of = factor_of * one(*cut)
    return factor_of


def bell_draw(key, shape, spread, reach, shards=(), kind=jnp.bfloat16):
    loudness = block_levels(key, shape, shards, -0.22, 0.18) if shards else 1.0
    values = jax.random.normal(key, shape, jnp.float32) * spread * loudness
    return jnp.minimum(jnp.maximum(values, -reach), reach).astype(kind)


def setup_inputs(seed: int = 0) -> dict:
    splits = jax.random.split(jax.random.key(seed), 17)
    hidden = bell_draw(splits[0], (TOKENS, D), 1.0, 6.0, ((0, 8),))
    cotangent = bell_draw(splits[1], (TOKENS, D), 1.0, 6.0, ((0, 8),))
    norm_gain = jnp.clip(1.0 + 0.1 * jax.random.normal(splits[2], (D,), jnp.float32), 0.5, 1.5)
    gate_weight = bell_draw(splits[3], (D, INNER), D ** -0.5, 0.1875, ((1, 4),))
    value_weight = bell_draw(splits[4], (D, INNER), D ** -0.5, 0.1875, ((1, 4),))
    step_weight = bell_draw(splits[5], (D, HEADS), D ** -0.5, 0.1875, ((1, 4),))
    state_weight = bell_draw(splits[6], (D, 2 * STATE), D ** -0.5, 0.1875)
    value_kernel = bell_draw(splits[7], (CONV, INNER), CONV ** -0.5, 3.0, ((1, 4),), jnp.float32)
    value_offset = bell_draw(splits[8], (INNER,), 0.5, 3.0, ((0, 4),), jnp.float32)
    state_kernel = bell_draw(splits[9], (CONV, 2 * STATE), CONV ** -0.5, 3.0, (), jnp.float32)
    state_offset = bell_draw(splits[10], (2 * STATE,), 0.5, 3.0, (), jnp.float32)
    step_offset = jnp.clip(-6.5 + 4.0 * jax.random.uniform(splits[11], (HEADS,), jnp.float32) ** block_levels(splits[11], (HEADS,), ((0, 4),), -0.2, 0.2), -6.5, -2.5)
    log_decay = jnp.clip(2.8 * jax.random.uniform(splits[12], (HEADS,), jnp.float32) ** block_levels(splits[12], (HEADS,), ((0, 4),), -0.2, 0.2), 0.0, 2.8)
    skip_gain = jnp.clip(0.5 + 1.0 * jax.random.uniform(splits[13], (HEADS,), jnp.float32) ** block_levels(splits[13], (HEADS,), ((0, 4),), -0.2, 0.2), 0.5, 1.5)
    mixer_gain = jnp.clip(1.0 + 0.1 * jax.random.normal(splits[14], (INNER,), jnp.float32), 0.5, 1.5)
    output_weight = bell_draw(splits[15], (INNER, D), INNER ** -0.5, 0.125, ((0, 4),))
    return dict(hidden=hidden, cotangent=cotangent, norm_gain=norm_gain, gate_weight=gate_weight, value_weight=value_weight, step_weight=step_weight, state_weight=state_weight, value_kernel=value_kernel, value_offset=value_offset, state_kernel=state_kernel, state_offset=state_offset, step_offset=step_offset, log_decay=log_decay, skip_gain=skip_gain, mixer_gain=mixer_gain, output_weight=output_weight)


epsilon = 1e-05
highest = lax.Precision.HIGHEST

@jax.custom_vjp
def low(v):
    return lax.optimization_barrier(v.astype(jnp.bfloat16)).astype(jnp.float32)

@jax.custom_vjp
def low_back(v):
    return v

def low_keep(v):
    return (low(v), None)

def low_pass(kept, grad):
    return (grad,)

def back_keep(v):
    return (v, None)

def back_low(kept, grad):
    return (low(grad),)
low.defvjp(low_keep, low_pass)
low_back.defvjp(back_keep, back_low)

def matmul(left, right):
    return jnp.dot(left, right, precision=highest, preferred_element_type=jnp.float32)

def causal(values, kernel, offset):
    channels = values.shape[1]
    blocks = values.reshape(-1, SEQ_LEN, channels)
    padded = jnp.pad(blocks, ((0, 0), (CONV - 1, 0), (0, 0)))
    total = offset + kernel[0] * padded[:, 0:SEQ_LEN]
    for position in range(1, CONV):
        total = total + kernel[position] * padded[:, position:position + SEQ_LEN]
    return jax.nn.silu(total).reshape(-1, channels)

def scan_sequence(inputs, timing, writer, reader, decay_rate, skip_gain):
    length, width = inputs.shape
    heads = timing.shape[1]
    groups = length // GROUP
    blocked = inputs.reshape(groups, GROUP, heads, width // heads)
    steps_block = timing.reshape(groups, GROUP, heads)
    writes = writer.reshape(groups, GROUP, -1)
    reads = reader.reshape(groups, GROUP, -1)
    logs = jnp.cumsum(steps_block * decay_rate, axis=1).transpose(0, 2, 1)
    steps_heads = steps_block.transpose(0, 2, 1)
    scores = jnp.einsum('cin,cjn->cij', reads, writes, precision=highest)
    rows = lax.broadcasted_iota(jnp.int32, (GROUP, GROUP), 0)
    cols = lax.broadcasted_iota(jnp.int32, (GROUP, GROUP), 1)
    lower = rows >= cols
    decays = jnp.exp(jnp.where(lower, logs[:, :, :, None] - logs[:, :, None, :], -jnp.inf))
    weights = scores[:, None] * decays * steps_heads[:, :, None, :]
    inside = jnp.einsum('chij,cjhp->cihp', weights, blocked, precision=highest)
    tails = jnp.exp(logs[:, :, -1:] - logs) * steps_heads
    states = jnp.einsum('cjn,chj,cjhp->chnp', writes, tails, blocked, precision=highest)
    carries = jnp.exp(logs[:, :, -1])

    def advance(carry, pieces):
        return (pieces[0][:, None, None] * carry + pieces[1], carry)
    start = jnp.zeros((heads, writes.shape[2], width // heads), jnp.float32)
    unused, previous = lax.scan(advance, start, (carries, states))
    across = jnp.einsum('cin,chnp->cihp', reads, previous, precision=highest)
    across = across * jnp.exp(logs).transpose(0, 2, 1)[:, :, :, None]
    result = inside + across + skip_gain[None, None, :, None] * blocked
    return result.reshape(length, width)

def mixer(inputs, selects, step_raw, gate_raw, step_offset, log_decay, skip_gain):
    timing = jax.nn.softplus(step_raw + step_offset)
    decay_rate = -jnp.exp(log_decay)
    state_width = selects.shape[1] // 2
    width = inputs.shape[1]
    heads = timing.shape[1]

    def one_sequence(pieces):
        return scan_sequence(pieces[0], pieces[1], pieces[2], pieces[3], decay_rate, skip_gain)
    mixed = lax.map(jax.checkpoint(one_sequence), (inputs.reshape(-1, SEQ_LEN, width), timing.reshape(-1, SEQ_LEN, heads), selects[:, :state_width].reshape(-1, SEQ_LEN, state_width), selects[:, state_width:].reshape(-1, SEQ_LEN, state_width)))
    return mixed.reshape(-1, width) * jax.nn.silu(gate_raw)

def forward(hidden, norm_gain, gate_weight, value_weight, step_weight, state_weight, value_kernel, value_offset, state_kernel, state_offset, step_offset, log_decay, skip_gain, mixer_gain, output_weight):
    recip = lax.rsqrt(lax.optimization_barrier(jnp.mean(hidden * hidden, axis=1, keepdims=True)) + epsilon)
    normed = low(hidden * recip * norm_gain)
    gate_raw = low_back(matmul(normed, gate_weight))
    value_raw = low_back(matmul(normed, value_weight))
    step_raw = low_back(matmul(normed, step_weight))
    select_raw = low_back(matmul(normed, state_weight))
    inputs = low(causal(value_raw, value_kernel, value_offset))
    selects = low(causal(select_raw, state_kernel, state_offset))
    gated = mixer(inputs, selects, step_raw, gate_raw, step_offset, log_decay, skip_gain)
    scale = lax.rsqrt(lax.optimization_barrier(jnp.mean(gated * gated, axis=1, keepdims=True)) + epsilon)
    update = low(gated * mixer_gain)
    return hidden + low_back(matmul(update, output_weight)) * scale

def reference(hidden, cotangent, norm_gain, gate_weight, value_weight, step_weight, state_weight, value_kernel, value_offset, state_kernel, state_offset, step_offset, log_decay, skip_gain, mixer_gain, output_weight):
    output, pullback = jax.vjp(forward, hidden.astype(jnp.float32), norm_gain, gate_weight.astype(jnp.float32), value_weight.astype(jnp.float32), step_weight.astype(jnp.float32), state_weight.astype(jnp.float32), value_kernel, value_offset, state_kernel, state_offset, step_offset, log_decay, skip_gain, mixer_gain, output_weight.astype(jnp.float32))
    grads = pullback(cotangent.astype(jnp.float32))
    return (output.astype(jnp.bfloat16), grads[0], grads[1], grads[2], grads[3], grads[4], grads[5], grads[6], grads[7], grads[8], grads[9], grads[10], grads[11], grads[12], grads[13], grads[14])
```

```python
import jax
import jax.numpy as jnp
from jax import lax
from jax.sharding import PartitionSpec as P

D = 1024
CONV = 4
GROUP = 256
SEQ_LEN = 1024
INNER = 2048


epsilon = 1e-05
highest = lax.Precision.HIGHEST


def plain(left, right):
    return jnp.dot(left, right, preferred_element_type=jnp.float32)


def back_product(grads, weight):
    return lax.dot_general(
        grads, weight, (((1,), (1,)), ((), ())), preferred_element_type=jnp.float32
    )


def weight_product(left, right):
    return lax.dot_general(
        left, right, (((0,), (0,)), ((), ())), preferred_element_type=jnp.float32
    )


def rounded(values):
    return lax.optimization_barrier(values.astype(jnp.bfloat16)).astype(jnp.float32)


def causal(values, kernel, offset):
    channels = values.shape[1]
    blocks = values.reshape(-1, SEQ_LEN, channels)
    padded = jnp.pad(blocks, ((0, 0), (CONV - 1, 0), (0, 0)))
    total = offset + kernel[0] * padded[:, 0:SEQ_LEN]
    for position in range(1, CONV):
        total = total + kernel[position] * padded[:, position : position + SEQ_LEN]
    return jax.nn.silu(total).reshape(-1, channels)


def both_convs(value_raw, select_raw, value_kernel, value_offset, state_kernel, state_offset):
    return (
        causal(value_raw, value_kernel, value_offset),
        causal(select_raw, state_kernel, state_offset),
    )


def scan_sequence(inputs, timing, writer, reader, decay_rate, skip_gain):
    length, width = inputs.shape
    heads = timing.shape[1]
    groups = length // GROUP
    blocked = inputs.reshape(groups, GROUP, heads, width // heads)
    steps_block = timing.reshape(groups, GROUP, heads)
    writes = writer.reshape(groups, GROUP, -1)
    reads = reader.reshape(groups, GROUP, -1)
    logs = jnp.cumsum(steps_block * decay_rate, axis=1).transpose(0, 2, 1)
    steps_heads = steps_block.transpose(0, 2, 1)
    scores = jnp.einsum("cin,cjn->cij", reads, writes, precision=highest)
    rows = lax.broadcasted_iota(jnp.int32, (GROUP, GROUP), 0)
    cols = lax.broadcasted_iota(jnp.int32, (GROUP, GROUP), 1)
    lower = rows >= cols
    decays = jnp.exp(jnp.where(lower, logs[:, :, :, None] - logs[:, :, None, :], -jnp.inf))
    weights = scores[:, None] * decays * steps_heads[:, :, None, :]
    inside = jnp.einsum("chij,cjhp->cihp", weights, blocked, precision=highest)
    tails = jnp.exp(logs[:, :, -1:] - logs) * steps_heads
    states = jnp.einsum("cjn,chj,cjhp->chnp", writes, tails, blocked, precision=highest)
    carries = jnp.exp(logs[:, :, -1])

    def advance(carry, pieces):
        return (pieces[0][:, None, None] * carry + pieces[1], carry)

    start = jnp.zeros((heads, writes.shape[2], width // heads), jnp.float32)
    unused, previous = lax.scan(advance, start, (carries, states))
    across = jnp.einsum("cin,chnp->cihp", reads, previous, precision=highest)
    across = across * jnp.exp(logs).transpose(0, 2, 1)[:, :, :, None]
    result = inside + across + skip_gain[None, None, :, None] * blocked
    return result.reshape(length, width)


def mixer(inputs, selects, step_raw, gate_raw, step_offset, log_decay, skip_gain):
    timing = jax.nn.softplus(step_raw + step_offset)
    decay_rate = -jnp.exp(log_decay)
    state_width = selects.shape[1] // 2
    width = inputs.shape[1]
    heads = timing.shape[1]

    def one_sequence(pieces):
        return scan_sequence(pieces[0], pieces[1], pieces[2], pieces[3], decay_rate, skip_gain)

    if inputs.shape[0] == SEQ_LEN:
        mixed = one_sequence(
            (inputs, timing, selects[:, :state_width], selects[:, state_width:])
        )
        return mixed * jax.nn.silu(gate_raw)

    mixed = lax.map(
        jax.checkpoint(one_sequence),
        (
            inputs.reshape(-1, SEQ_LEN, width),
            timing.reshape(-1, SEQ_LEN, heads),
            selects[:, :state_width].reshape(-1, SEQ_LEN, state_width),
            selects[:, state_width:].reshape(-1, SEQ_LEN, state_width),
        ),
    )
    return mixed.reshape(-1, width) * jax.nn.silu(gate_raw)


def swap(values, bit):
    count = lax.axis_size("tensor")
    return lax.ppermute(values, "tensor", [(i, i ^ bit) for i in range(count)])


def tensor_sum_small(values):
    bit = 1
    while bit < lax.axis_size("tensor"):
        values = values + swap(values, bit)
        bit *= 2
    return values


def halves(values, bit):
    half = values.shape[0] // 2
    upper = (lax.axis_index("tensor") & bit) // bit
    mine = lax.dynamic_slice_in_dim(values, upper * half, half)
    other = lax.dynamic_slice_in_dim(values, (1 - upper) * half, half)
    return mine, other


def joined(mine, other, bit):
    upper = (lax.axis_index("tensor") & bit) // bit
    half = mine.shape[0]
    whole = jnp.zeros((2 * half,) + mine.shape[1:], mine.dtype)
    whole = lax.dynamic_update_slice_in_dim(whole, mine, upper * half, 0)
    return lax.dynamic_update_slice_in_dim(whole, other, (1 - upper) * half, 0)


def tensor_scatter(values):
    bit = 1
    while bit < lax.axis_size("tensor"):
        mine, other = halves(values, bit)
        values = mine + swap(other, bit)
        bit *= 2
    return values


def tensor_gather(values):
    bit = lax.axis_size("tensor") // 2
    while bit:
        values = joined(values, swap(values, bit), bit)
        bit //= 2
    return values


def tensor_sum(values):
    mine, other = halves(values, 1)
    mine = mine + swap(other, 1)
    bit = 2
    while bit < lax.axis_size("tensor"):
        mine = mine + swap(mine, bit)
        bit *= 2
    return joined(mine, swap(mine, 1), 1)


def ring_sum(values):
    n = lax.axis_size("dp")
    if n > 8 or n % 2:
        return lax.psum(values, "dp")
    order = list(range(0, n, 2)) + list(range(n - 1, 0, -2))
    places = [0] * n
    for place, device in enumerate(order):
        places[device] = place
    me = jnp.array(places, jnp.int32)[lax.axis_index("dp")]
    ahead = [(order[i], order[(i + 1) % n]) for i in range(n)]
    behind = [(b, a) for a, b in ahead]
    rows = values.shape[0] // (2 * n)
    tail = (0,) * (values.ndim - 1)

    def start(place, side):
        return (2 * ((place + 2 * n) % n) + side) * rows

    def take(place, side):
        return lax.dynamic_slice_in_dim(values, start(place, side), rows)

    front, back = take(me, 0), take(me, 1)
    for step in range(1, n):
        front = lax.ppermute(front, "dp", ahead) + take(me - step, 0)
        back = lax.ppermute(back, "dp", behind) + take(me + step, 1)
    whole = values
    for step in range(n):
        whole = lax.dynamic_update_slice(whole, front, (start(me + 1 - step, 0),) + tail)
        whole = lax.dynamic_update_slice(whole, back, (start(me - 1 + step, 1),) + tail)
        if step < n - 1:
            front = lax.ppermute(front, "dp", ahead)
            back = lax.ppermute(back, "dp", behind)
    return whole


def packed(parts, multiple):
    flat = jnp.concatenate([part.reshape(-1) for part in parts])
    return jnp.pad(flat, (0, -flat.shape[0] % multiple))


def unpacked(flat, parts):
    results, at = [], 0
    for part in parts:
        results.append(flat[at : at + part.size].reshape(part.shape))
        at += part.size
    return results


def body(
    hidden,
    cotangent,
    norm_gain,
    gate_weight,
    value_weight,
    step_weight,
    state_weight,
    value_kernel,
    value_offset,
    state_kernel,
    state_offset,
    step_offset,
    log_decay,
    skip_gain,
    mixer_gain,
    output_weight,
):
    source = hidden.astype(jnp.float32)
    recip = lax.rsqrt(jnp.mean(source * source, axis=1, keepdims=True) + epsilon)
    scaled = source * recip
    normed = (scaled * norm_gain).astype(jnp.bfloat16)
    gate_raw = plain(normed, gate_weight)
    value_raw = plain(normed, value_weight)
    step_raw = plain(normed, step_weight)
    select_raw = plain(normed, state_weight)
    (conv_values, conv_selects), conv_back = jax.vjp(
        both_convs, value_raw, select_raw, value_kernel, value_offset, state_kernel, state_offset
    )
    inputs = rounded(conv_values)
    selects = rounded(conv_selects)
    gated, mixer_back = jax.vjp(
        mixer, inputs, selects, step_raw, gate_raw, step_offset, log_decay, skip_gain
    )
    local_squares = jnp.sum(gated * gated, axis=1)
    update = (gated * mixer_gain).astype(jnp.bfloat16)
    branch_part = plain(update, output_weight)
    upstream = cotangent.astype(jnp.float32)
    local_dots = jnp.sum(upstream * branch_part, axis=1)
    squares, d_scale = tensor_sum_small(jnp.stack([local_squares, local_dots]))
    d_scale = d_scale[:, None]
    projected = tensor_sum(branch_part)
    scale = lax.rsqrt(squares / INNER + epsilon)[:, None]
    output = (source + projected * scale).astype(jnp.bfloat16)
    d_projected = (upstream * scale).astype(jnp.bfloat16)
    output_grad = weight_product(update, d_projected)
    d_update = back_product(d_projected, output_weight)
    mixing_grad = jnp.sum(d_update * gated, axis=0)
    d_gated = d_update * mixer_gain - d_scale * scale**3 * gated / INNER
    d_inputs, d_selects, d_step, d_gate, timing_grad, decay_grad, skip_grad = mixer_back(d_gated)
    d_value, d_select, kernel_grad, offset_grad, filter_part, shift_part = conv_back(
        (d_inputs, d_selects)
    )
    gate_low = d_gate.astype(jnp.bfloat16)
    value_low = d_value.astype(jnp.bfloat16)
    step_low = d_step.astype(jnp.bfloat16)
    select_low = d_select.astype(jnp.bfloat16)
    normed_part = back_product(gate_low, gate_weight) + back_product(value_low, value_weight)
    normed_part = (
        normed_part + back_product(step_low, step_weight) + back_product(select_low, state_weight)
    )
    d_normed = tensor_sum(normed_part)
    gate_grad = weight_product(normed, gate_low)
    value_grad = weight_product(normed, value_low)
    step_grad = weight_product(normed, step_low)
    state_part = weight_product(normed, select_low)
    gain_grad = jnp.sum(normed_part * scaled, axis=0)
    d_scaled = d_normed * norm_gain
    d_recip = jnp.sum(d_scaled * source, axis=1, keepdims=True)
    hidden_grad = upstream + d_scaled * recip - d_recip * recip**3 * source / D
    output_grad = ring_sum(output_grad)
    gate_grad = ring_sum(gate_grad)
    value_grad = ring_sum(value_grad)
    shared = [state_part, gain_grad, filter_part, shift_part]
    own = [step_grad, kernel_grad, offset_grad, timing_grad, decay_grad, skip_grad, mixing_grad]
    lane = 128
    shares = lax.axis_size("tensor")
    quarter = tensor_scatter(packed(shared, 8 * lane * shares).reshape(-1, lane))
    summed = ring_sum(packed([quarter] + own, 16 * 8 * lane).reshape(-1, lane)).reshape(-1)
    quarter, *own = unpacked(summed, [quarter] + own)
    step_grad, kernel_grad, offset_grad, timing_grad, decay_grad, skip_grad, mixing_grad = own
    state_grad, gain_grad, filter_grad, shift_grad = unpacked(tensor_gather(quarter).reshape(-1), shared)
    return (
        output,
        hidden_grad,
        gain_grad,
        gate_grad,
        value_grad,
        step_grad,
        state_grad,
        kernel_grad,
        offset_grad,
        filter_grad,
        shift_grad,
        timing_grad,
        decay_grad,
        skip_grad,
        mixing_grad,
        output_grad,
    )


def solution(mesh):
    return jax.shard_map(
        body,
        mesh=mesh,
        in_specs=(
            P("dp", None),
            P("dp", None),
            P(),
            P(None, "tensor"),
            P(None, "tensor"),
            P(None, "tensor"),
            P(),
            P(None, "tensor"),
            P("tensor"),
            P(),
            P(),
            P("tensor"),
            P("tensor"),
            P("tensor"),
            P("tensor"),
            P("tensor", None),
        ),
        out_specs=(
            P("dp", None),
            P("dp", None),
            P(),
            P(None, "tensor"),
            P(None, "tensor"),
            P(None, "tensor"),
            P(),
            P(None, "tensor"),
            P("tensor"),
            P(),
            P(),
            P("tensor"),
            P("tensor"),
            P("tensor"),
            P("tensor"),
            P("tensor", None),
        ),
        check_vma=False,
    )
```

```python
import jax
import jax.numpy as jnp
from jax import lax
from jax.experimental import pallas as pl
from jax.experimental.pallas import tpu as pltpu
from jax.sharding import PartitionSpec as P

D = 1024
CONV = 4
GROUP = 256
SEQ_LEN = 1024
INNER = 2048


epsilon = 1e-05
highest = lax.Precision.HIGHEST


def plain(left, right):
    return jnp.dot(left, right, preferred_element_type=jnp.float32)


def back_product(grads, weight):
    return lax.dot_general(
        grads, weight, (((1,), (1,)), ((), ())), preferred_element_type=jnp.float32
    )


def weight_product(left, right):
    return lax.dot_general(
        left, right, (((0,), (0,)), ((), ())), preferred_element_type=jnp.float32
    )


def causal(values, kernel, offset):
    channels = values.shape[1]
    blocks = values.reshape(-1, SEQ_LEN, channels)
    padded = jnp.pad(blocks, ((0, 0), (CONV - 1, 0), (0, 0)))
    total = offset + kernel[0] * padded[:, 0:SEQ_LEN]
    for position in range(1, CONV):
        total = total + kernel[position] * padded[:, position : position + SEQ_LEN]
    return jax.nn.silu(total).reshape(-1, channels)


def both_convs(value_raw, select_raw, value_kernel, value_offset, state_kernel, state_offset):
    return (
        causal(value_raw, value_kernel, value_offset),
        causal(select_raw, state_kernel, state_offset),
    )


def mixed_dot(left, right, dims=((1,), (0,))):
    return lax.dot_general(
        left.astype(jnp.bfloat16),
        right.astype(jnp.bfloat16),
        (dims, ((), ())),
        preferred_element_type=jnp.float32,
    )


def exact_dot(left, right, dims=((1,), (0,))):
    return lax.dot_general(
        left, right, (dims, ((), ())), precision=highest, preferred_element_type=jnp.float32
    )


def spread(columns, width):
    rows, heads = columns.shape
    return jnp.concatenate(
        [jnp.broadcast_to(columns[:, h : h + 1], (rows, width)) for h in range(heads)], axis=1
    )


def block_logs(steps, steps_flat, rate, rate_flat):
    rows = lax.broadcasted_iota(jnp.int32, (GROUP, GROUP), 0)
    cols = lax.broadcasted_iota(jnp.int32, (GROUP, GROUP), 1)
    lower = rows >= cols
    ones = jnp.where(lower, 1.0, 0.0).astype(jnp.float32)
    logs = exact_dot(ones, steps * rate)
    logs_flat = exact_dot(steps_flat * rate_flat, ones, ((1,), (1,)))
    return lower, ones, logs, logs_flat


def forward_kernel(
    x_ref, steps_ref, flat_ref, rate_ref, rate_flat_ref, select_ref, skip_ref, gate_ref, gain_ref,
    scanned_ref, states_ref, update_ref, squares_ref, state,
):
    @pl.when(pl.program_id(0) == 0)
    def clear():
        state[...] = jnp.zeros_like(state)

    width = x_ref.shape[1] // steps_ref.shape[1]
    states_ref[0] = state[...]
    x = x_ref[...]
    steps, flat = steps_ref[...], flat_ref[...]
    lower, unused, logs, logs_flat = block_logs(steps, flat, rate_ref[...], rate_flat_ref[...])
    half = select_ref.shape[1] // 2
    writes, reads = select_ref[:, :half], select_ref[:, half:]
    scores = mixed_dot(reads, writes, ((1,), (1,)))
    last = logs[GROUP - 1 : GROUP, :]
    tails = jnp.exp(last - logs) * steps
    wide = x.astype(jnp.float32)
    across = mixed_dot(reads, state[...]) * spread(jnp.exp(logs), width)
    insides = []
    for h in range(steps.shape[1]):
        decays = jnp.exp(jnp.where(lower, logs[:, h : h + 1] - logs_flat[h : h + 1, :], -1e30))
        weights = scores * decays * flat[h : h + 1, :]
        insides.append(mixed_dot(weights, x[:, h * width : (h + 1) * width]))
    scanned = jnp.concatenate(insides, axis=1) + across + skip_ref[...] * wide
    state[...] = state[...] * spread(jnp.exp(last), width) + mixed_dot(
        writes, wide * spread(tails, width), ((0,), (0,))
    )
    gate = gate_ref[...]
    gated = scanned * (gate / (1.0 + jnp.exp(-gate)))
    scanned_ref[...] = scanned
    update_ref[...] = (gated * gain_ref[...]).astype(jnp.bfloat16)
    squares_ref[...] = jnp.sum(gated * gated, axis=1, keepdims=True)


def backward_kernel(
    x_ref, steps_ref, flat_ref, rate_ref, rate_flat_ref, select_ref, skip_ref, gate_ref, gain_ref,
    scanned_ref, states_ref, d_update_ref, factor_ref,
    d_x_ref, d_select_ref, d_steps_ref, d_gate_ref, d_rate_ref, d_skip_ref, d_gain_ref, carry,
):
    @pl.when(pl.program_id(0) == 0)
    def clear():
        carry[...] = jnp.zeros_like(carry)
        d_rate_ref[...] = jnp.zeros_like(d_rate_ref)
        d_skip_ref[...] = jnp.zeros_like(d_skip_ref)
        d_gain_ref[...] = jnp.zeros_like(d_gain_ref)

    heads = steps_ref.shape[1]
    width = x_ref.shape[1] // heads
    x = x_ref[...]
    wide = x.astype(jnp.float32)
    steps, flat, rate = steps_ref[...], flat_ref[...], rate_ref[...]
    lower, ones, logs, logs_flat = block_logs(steps, flat, rate, rate_flat_ref[...])
    half = select_ref.shape[1] // 2
    writes, reads = select_ref[:, :half], select_ref[:, half:]
    gate, scanned, d_update = gate_ref[...], scanned_ref[...], d_update_ref[...]
    sigmoid = 1.0 / (1.0 + jnp.exp(-gate))
    gated = scanned * (gate * sigmoid)
    d_gain_ref[...] += jnp.sum(d_update * gated, axis=0, keepdims=True)
    d_gated = d_update * gain_ref[...] - factor_ref[...] * gated
    d_gate = d_gated * scanned * (sigmoid * (1.0 + gate * (1.0 - sigmoid)))
    d_gate_ref[...] = d_gate.astype(jnp.bfloat16)
    grads = d_gated * (gate * sigmoid)
    grads_low = grads.astype(jnp.bfloat16)
    d_skip_ref[...] += jnp.sum(grads * wide, axis=0, keepdims=True)
    scores = mixed_dot(reads, writes, ((1,), (1,)))
    last = logs[GROUP - 1 : GROUP, :]
    fades = jnp.exp(last - logs)
    tails = fades * steps
    ends = jnp.exp(last)
    before, after = states_ref[0], carry[...]
    before_low, after_low = before.astype(jnp.bfloat16), after.astype(jnp.bfloat16)
    grown = jnp.exp(logs)
    scaled = grads * spread(grown, width)
    across = mixed_dot(reads, before_low) * scaled
    back = mixed_dot(writes, after_low)
    tails_wide = spread(tails, width)
    touched = wide * back
    d_reads = mixed_dot(scaled, before_low, ((1,), (1,)))
    d_writes = mixed_dot(wide * tails_wide, after_low, ((1,), (1,)))
    products = jnp.sum(before * after, axis=0, keepdims=True)
    carry[...] = after * spread(ends, width) + mixed_dot(reads, scaled, ((0,), (0,)))
    d_scores = jnp.zeros((GROUP, GROUP), jnp.float32)
    head_ids = lax.broadcasted_iota(jnp.int32, (1, heads), 1)
    row_ids = lax.broadcasted_iota(jnp.int32, (heads, 1), 0)
    row_sums = jnp.zeros((GROUP, heads), jnp.float32)
    d_tails = jnp.zeros((GROUP, heads), jnp.float32)
    d_ends = jnp.zeros((1, heads), jnp.float32)
    col_sums = jnp.zeros((heads, GROUP), jnp.float32)
    insides = []
    for h in range(heads):
        at = slice(h * width, (h + 1) * width)
        row = flat[h : h + 1, :]
        decays = jnp.exp(jnp.where(lower, logs[:, h : h + 1] - logs_flat[h : h + 1, :], -1e30))
        d_weights = mixed_dot(grads_low[:, at], x[:, at], ((1,), (1,)))
        kept = scores * decays
        insides.append(mixed_dot(kept * row, grads_low[:, at], ((0,), (0,))))
        d_scores = d_scores + d_weights * (decays * row)
        reach = d_weights * kept
        sums = jnp.sum(reach * row, axis=1, keepdims=True)
        sums = sums + jnp.sum(across[:, at], axis=1, keepdims=True)
        mine = head_ids == h
        row_sums = jnp.where(mine, sums, row_sums)
        col_sums = jnp.where(row_ids == h, jnp.sum(reach, axis=0, keepdims=True), col_sums)
        d_tails = jnp.where(mine, jnp.sum(touched[:, at], axis=1, keepdims=True), d_tails)
        d_ends = jnp.where(mine, jnp.sum(products[:, at], axis=1, keepdims=True), d_ends)
    corner = jnp.where(
        lax.broadcasted_iota(jnp.int32, (heads, heads), 0)
        == lax.broadcasted_iota(jnp.int32, (heads, heads), 1),
        1.0,
        0.0,
    ).astype(jnp.float32)
    reached = exact_dot(col_sums, corner, ((0,), (0,)))
    pulled = d_tails * tails
    d_last = d_ends * ends + jnp.sum(pulled, axis=0, keepdims=True)
    d_logs = row_sums - reached * steps - pulled
    d_rates = exact_dot(ones, d_logs, ((0,), (0,))) + d_last
    d_rate_ref[...] += jnp.sum(d_rates * steps, axis=0, keepdims=True)
    d_steps_ref[...] = d_rates * rate + reached + d_tails * fades
    d_x_ref[...] = (
        jnp.concatenate(insides, axis=1) + tails_wide * back + skip_ref[...] * grads
    )
    d_scores = d_scores.astype(jnp.bfloat16)
    d_select_ref[:, :half] = d_writes + mixed_dot(d_scores, reads, ((0,), (0,)))
    d_select_ref[:, half:] = d_reads + mixed_dot(d_scores, writes)


def kernel_specs(tokens, inner, heads, states, reverse):
    count = tokens // GROUP

    def at(i):
        return count - 1 - i if reverse else i

    def rows(cols):
        return pl.BlockSpec((GROUP, cols), lambda i: (at(i), 0))

    def fixed(height, cols):
        return pl.BlockSpec((height, cols), lambda i: (0, 0))

    shared = [
        rows(inner),
        rows(heads),
        pl.BlockSpec((heads, GROUP), lambda i: (0, at(i))),
        fixed(1, heads),
        fixed(heads, 1),
        rows(2 * states),
        fixed(1, inner),
        rows(inner),
        fixed(1, inner),
    ]
    kept = pl.BlockSpec((1, states, inner), lambda i: (at(i), 0, 0))
    return count, rows, fixed, shared, kept


def shape(dims, kind=jnp.float32):
    return jax.ShapeDtypeStruct(dims, kind)


def scan_forward(shared):
    tokens, inner = shared[0].shape
    heads, states = shared[1].shape[1], shared[5].shape[1] // 2
    count, rows, fixed, specs, kept = kernel_specs(SEQ_LEN, inner, heads, states, False)
    return pl.pallas_call(
        forward_kernel,
        grid=(count,),
        in_specs=specs,
        out_specs=[rows(inner), kept, rows(inner), rows(1)],
        out_shape=[
            shape((tokens, inner)),
            shape((count, states, inner)),
            shape((tokens, inner), jnp.bfloat16),
            shape((tokens, 1)),
        ],
        scratch_shapes=[pltpu.VMEM((states, inner), jnp.float32)],
    )(*shared)


def scan_backward(shared, scanned, kept_states, d_update, factor):
    tokens, inner = shared[0].shape
    heads, states = shared[1].shape[1], shared[5].shape[1] // 2
    count, rows, fixed, specs, kept = kernel_specs(SEQ_LEN, inner, heads, states, True)
    return pl.pallas_call(
        backward_kernel,
        grid=(count,),
        in_specs=specs + [rows(inner), kept, rows(inner), rows(1)],
        out_specs=[
            rows(inner), rows(2 * states), rows(heads), rows(inner),
            fixed(1, heads), fixed(1, inner), fixed(1, inner),
        ],
        out_shape=[
            shape((tokens, inner)), shape((tokens, 2 * states)), shape((tokens, heads)),
            shape((tokens, inner), jnp.bfloat16),
            shape((1, heads)), shape((1, inner)), shape((1, inner)),
        ],
        scratch_shapes=[pltpu.VMEM((states, inner), jnp.float32)],
    )(*shared, scanned, kept_states, d_update, factor)


def swap(values, bit):
    count = lax.axis_size("tensor")
    return lax.ppermute(values, "tensor", [(i, i ^ bit) for i in range(count)])


def tensor_sum_small(values):
    bit = 1
    while bit < lax.axis_size("tensor"):
        values = values + swap(values, bit)
        bit *= 2
    return values


def halves(values, bit):
    half = values.shape[0] // 2
    upper = (lax.axis_index("tensor") & bit) // bit
    mine = lax.dynamic_slice_in_dim(values, upper * half, half)
    other = lax.dynamic_slice_in_dim(values, (1 - upper) * half, half)
    return mine, other


def joined(mine, other, bit):
    upper = (lax.axis_index("tensor") & bit) // bit
    half = mine.shape[0]
    whole = jnp.zeros((2 * half,) + mine.shape[1:], mine.dtype)
    whole = lax.dynamic_update_slice_in_dim(whole, mine, upper * half, 0)
    return lax.dynamic_update_slice_in_dim(whole, other, (1 - upper) * half, 0)


def tensor_scatter(values):
    bit = 1
    while bit < lax.axis_size("tensor"):
        mine, other = halves(values, bit)
        values = mine + swap(other, bit)
        bit *= 2
    return values


def tensor_gather(values):
    bit = lax.axis_size("tensor") // 2
    while bit:
        values = joined(values, swap(values, bit), bit)
        bit //= 2
    return values


def tensor_sum(values):
    mine, other = halves(values, 1)
    mine = mine + swap(other, 1)
    bit = 2
    while bit < lax.axis_size("tensor"):
        mine = mine + swap(mine, bit)
        bit *= 2
    return joined(mine, swap(mine, 1), 1)


def ring_sum(values):
    n = lax.axis_size("dp")
    if n > 8 or n % 2:
        return lax.psum(values, "dp")
    order = list(range(0, n, 2)) + list(range(n - 1, 0, -2))
    places = [0] * n
    for place, device in enumerate(order):
        places[device] = place
    me = jnp.array(places, jnp.int32)[lax.axis_index("dp")]
    ahead = [(order[i], order[(i + 1) % n]) for i in range(n)]
    behind = [(b, a) for a, b in ahead]
    rows = values.shape[0] // (2 * n)
    tail = (0,) * (values.ndim - 1)

    def start(place, side):
        return (2 * ((place + 2 * n) % n) + side) * rows

    def take(place, side):
        return lax.dynamic_slice_in_dim(values, start(place, side), rows)

    front, back = take(me, 0), take(me, 1)
    for step in range(1, n):
        front = lax.ppermute(front, "dp", ahead) + take(me - step, 0)
        back = lax.ppermute(back, "dp", behind) + take(me + step, 1)
    whole = values
    for step in range(n):
        whole = lax.dynamic_update_slice(whole, front, (start(me + 1 - step, 0),) + tail)
        whole = lax.dynamic_update_slice(whole, back, (start(me - 1 + step, 1),) + tail)
        if step < n - 1:
            front = lax.ppermute(front, "dp", ahead)
            back = lax.ppermute(back, "dp", behind)
    return whole


def packed(parts, multiple):
    flat = jnp.concatenate([part.reshape(-1) for part in parts])
    return jnp.pad(flat, (0, -flat.shape[0] % multiple))


def unpacked(flat, parts):
    results, at = [], 0
    for part in parts:
        results.append(flat[at : at + part.size].reshape(part.shape))
        at += part.size
    return results


def body(
    hidden,
    cotangent,
    norm_gain,
    gate_weight,
    value_weight,
    step_weight,
    state_weight,
    value_kernel,
    value_offset,
    state_kernel,
    state_offset,
    step_offset,
    log_decay,
    skip_gain,
    mixer_gain,
    output_weight,
):
    source = hidden.astype(jnp.float32)
    recip = lax.rsqrt(jnp.mean(source * source, axis=1, keepdims=True) + epsilon)
    scaled = source * recip
    normed = (scaled * norm_gain).astype(jnp.bfloat16)
    gate_raw = plain(normed, gate_weight)
    value_raw = plain(normed, value_weight)
    step_raw = plain(normed, step_weight)
    select_raw = plain(normed, state_weight)
    (conv_values, conv_selects), conv_back = jax.vjp(
        both_convs, value_raw, select_raw, value_kernel, value_offset, state_kernel, state_offset
    )
    inputs = conv_values.astype(jnp.bfloat16)
    selects = conv_selects.astype(jnp.bfloat16)
    step_total = step_raw + step_offset
    timing = jax.nn.softplus(step_total)
    decay_rate = -jnp.exp(log_decay)
    heads = timing.shape[1]
    width = inputs.shape[1] // heads
    shared_inputs = (
        inputs, timing, timing.T, decay_rate[None, :], decay_rate[:, None], selects,
        jnp.repeat(skip_gain, width)[None, :], gate_raw, mixer_gain[None, :],
    )
    scanned, kept_states, update, local_squares = scan_forward(shared_inputs)
    branch_part = plain(update, output_weight)
    upstream = cotangent.astype(jnp.float32)
    local_dots = jnp.sum(upstream * branch_part, axis=1)
    squares, d_scale = tensor_sum_small(jnp.stack([local_squares[:, 0], local_dots]))
    d_scale = d_scale[:, None]
    projected = tensor_sum(branch_part)
    scale = lax.rsqrt(squares / INNER + epsilon)[:, None]
    output = (source + projected * scale).astype(jnp.bfloat16)
    d_projected = (upstream * scale).astype(jnp.bfloat16)
    output_grad = weight_product(update, d_projected)
    d_update = back_product(d_projected, output_weight)
    factor = d_scale * scale**3 / INNER
    d_inputs, d_selects, d_timing, gate_low, d_rate, d_skip, d_gain = scan_backward(
        shared_inputs, scanned, kept_states, d_update, factor
    )
    d_step = d_timing * jax.nn.sigmoid(step_total)
    timing_grad = jnp.sum(d_step, axis=0)
    decay_grad = d_rate[0] * decay_rate
    skip_grad = jnp.sum(d_skip.reshape(heads, width), axis=1)
    mixing_grad = d_gain[0]
    d_value, d_select, kernel_grad, offset_grad, filter_part, shift_part = conv_back(
        (d_inputs, d_selects)
    )
    value_low = d_value.astype(jnp.bfloat16)
    step_low = d_step.astype(jnp.bfloat16)
    select_low = d_select.astype(jnp.bfloat16)
    normed_part = back_product(gate_low, gate_weight) + back_product(value_low, value_weight)
    normed_part = (
        normed_part + back_product(step_low, step_weight) + back_product(select_low, state_weight)
    )
    d_normed = tensor_sum(normed_part)
    both_grad = weight_product(normed, jnp.concatenate([gate_low, value_low], axis=1))
    step_grad = weight_product(normed, step_low)
    state_part = weight_product(normed, select_low)
    gain_grad = jnp.sum(normed_part * scaled, axis=0)
    d_scaled = d_normed * norm_gain
    d_recip = jnp.sum(d_scaled * source, axis=1, keepdims=True)
    hidden_grad = upstream + d_scaled * recip - d_recip * recip**3 * source / D
    output_grad = lax.psum(output_grad, "dp")
    both_grad = ring_sum(both_grad)
    gate_grad, value_grad = jnp.split(both_grad, 2, axis=1)
    shared = [state_part, gain_grad, filter_part, shift_part]
    own = [step_grad, kernel_grad, offset_grad, timing_grad, decay_grad, skip_grad, mixing_grad]
    lane = 128
    shares = lax.axis_size("tensor")
    quarter = tensor_scatter(packed(shared, 8 * lane * shares).reshape(-1, lane))
    summed = ring_sum(packed([quarter] + own, 16 * 8 * lane).reshape(-1, lane)).reshape(-1)
    quarter, *own = unpacked(summed, [quarter] + own)
    step_grad, kernel_grad, offset_grad, timing_grad, decay_grad, skip_grad, mixing_grad = own
    state_grad, gain_grad, filter_grad, shift_grad = unpacked(tensor_gather(quarter).reshape(-1), shared)
    return (
        output,
        hidden_grad,
        gain_grad,
        gate_grad,
        value_grad,
        step_grad,
        state_grad,
        kernel_grad,
        offset_grad,
        filter_grad,
        shift_grad,
        timing_grad,
        decay_grad,
        skip_grad,
        mixing_grad,
        output_grad,
    )


def solution(mesh):
    return jax.shard_map(
        body,
        mesh=mesh,
        in_specs=(
            P("dp", None),
            P("dp", None),
            P(),
            P(None, "tensor"),
            P(None, "tensor"),
            P(None, "tensor"),
            P(),
            P(None, "tensor"),
            P("tensor"),
            P(),
            P(),
            P("tensor"),
            P("tensor"),
            P("tensor"),
            P("tensor"),
            P("tensor", None),
        ),
        out_specs=(
            P("dp", None),
            P("dp", None),
            P(),
            P(None, "tensor"),
            P(None, "tensor"),
            P(None, "tensor"),
            P(),
            P(None, "tensor"),
            P("tensor"),
            P(),
            P(),
            P("tensor"),
            P("tensor"),
            P("tensor"),
            P("tensor"),
            P("tensor", None),
        ),
        check_vma=False,
    )
```

```python
import jax
import jax.numpy as jnp
from jax import lax
from jax.experimental import pallas as pl
from jax.experimental.pallas import tpu as pltpu
from jax.sharding import PartitionSpec as P

D = 1024
CONV = 4
GROUP = 256
SEQ_LEN = 1024
INNER = 2048


epsilon = 1e-05
highest = lax.Precision.HIGHEST


def plain(left, right):
    return jnp.dot(left, right, preferred_element_type=jnp.float32)


def back_product(grads, weight):
    return lax.dot_general(
        grads, weight, (((1,), (1,)), ((), ())), preferred_element_type=jnp.float32
    )


def weight_product(left, right):
    return lax.dot_general(
        left, right, (((0,), (0,)), ((), ())), preferred_element_type=jnp.float32
    )


def causal(values, kernel, offset):
    channels = values.shape[1]
    blocks = values.reshape(-1, SEQ_LEN, channels)
    padded = jnp.pad(blocks, ((0, 0), (CONV - 1, 0), (0, 0)))
    total = offset + kernel[0] * padded[:, 0:SEQ_LEN]
    for position in range(1, CONV):
        total = total + kernel[position] * padded[:, position : position + SEQ_LEN]
    return jax.nn.silu(total).reshape(-1, channels)


def both_convs(value_raw, select_raw, value_kernel, value_offset, state_kernel, state_offset):
    return (
        causal(value_raw, value_kernel, value_offset),
        causal(select_raw, state_kernel, state_offset),
    )


def mixed_dot(left, right, dims=((1,), (0,))):
    return lax.dot_general(
        left.astype(jnp.bfloat16),
        right.astype(jnp.bfloat16),
        (dims, ((), ())),
        preferred_element_type=jnp.float32,
    )


def exact_dot(left, right, dims=((1,), (0,))):
    return lax.dot_general(
        left, right, (dims, ((), ())), precision=highest, preferred_element_type=jnp.float32
    )


def spread(columns, width):
    rows, heads = columns.shape
    return jnp.concatenate(
        [jnp.broadcast_to(columns[:, h : h + 1], (rows, width)) for h in range(heads)], axis=1
    )


def block_logs(steps, steps_flat, rate, rate_flat):
    rows = lax.broadcasted_iota(jnp.int32, (GROUP, GROUP), 0)
    cols = lax.broadcasted_iota(jnp.int32, (GROUP, GROUP), 1)
    lower = rows >= cols
    ones = jnp.where(lower, 1.0, 0.0).astype(jnp.float32)
    logs = exact_dot(ones, steps * rate)
    logs_flat = exact_dot(steps_flat * rate_flat, ones, ((1,), (1,)))
    return lower, ones, logs, logs_flat


def forward_kernel(
    x_ref, steps_ref, flat_ref, rate_ref, rate_flat_ref, select_ref, skip_ref, gate_ref, gain_ref,
    scanned_ref, states_ref, update_ref, squares_ref, state,
):
    @pl.when(pl.program_id(0) == 0)
    def clear():
        state[...] = jnp.zeros_like(state)

    width = x_ref.shape[1] // steps_ref.shape[1]
    states_ref[0] = state[...]
    x = x_ref[...]
    steps, flat = steps_ref[...], flat_ref[...]
    lower, unused, logs, logs_flat = block_logs(steps, flat, rate_ref[...], rate_flat_ref[...])
    half = select_ref.shape[1] // 2
    writes, reads = select_ref[:, :half], select_ref[:, half:]
    scores = mixed_dot(reads, writes, ((1,), (1,)))
    last = logs[GROUP - 1 : GROUP, :]
    tails = jnp.exp(last - logs) * steps
    wide = x.astype(jnp.float32)
    across = mixed_dot(reads, state[...]) * spread(jnp.exp(logs), width)
    insides = []
    for h in range(steps.shape[1]):
        decays = jnp.exp(jnp.where(lower, logs[:, h : h + 1] - logs_flat[h : h + 1, :], -1e30))
        weights = scores * decays * flat[h : h + 1, :]
        insides.append(mixed_dot(weights, x[:, h * width : (h + 1) * width]))
    scanned = jnp.concatenate(insides, axis=1) + across + skip_ref[...] * wide
    state[...] = state[...] * spread(jnp.exp(last), width) + mixed_dot(
        writes, wide * spread(tails, width), ((0,), (0,))
    )
    gate = gate_ref[...]
    gated = scanned * (gate / (1.0 + jnp.exp(-gate)))
    scanned_ref[...] = scanned
    update_ref[...] = (gated * gain_ref[...]).astype(jnp.bfloat16)
    squares_ref[...] = jnp.sum(gated * gated, axis=1, keepdims=True)


def backward_kernel(
    x_ref, steps_ref, flat_ref, rate_ref, rate_flat_ref, select_ref, skip_ref, gate_ref, gain_ref,
    scanned_ref, states_ref, d_update_ref, factor_ref,
    d_x_ref, d_select_ref, d_steps_ref, d_gate_ref, d_rate_ref, d_skip_ref, d_gain_ref, carry,
):
    @pl.when(pl.program_id(0) == 0)
    def clear():
        carry[...] = jnp.zeros_like(carry)
        d_rate_ref[...] = jnp.zeros_like(d_rate_ref)
        d_skip_ref[...] = jnp.zeros_like(d_skip_ref)
        d_gain_ref[...] = jnp.zeros_like(d_gain_ref)

    heads = steps_ref.shape[1]
    width = x_ref.shape[1] // heads
    x = x_ref[...]
    wide = x.astype(jnp.float32)
    steps, flat, rate = steps_ref[...], flat_ref[...], rate_ref[...]
    lower, ones, logs, logs_flat = block_logs(steps, flat, rate, rate_flat_ref[...])
    half = select_ref.shape[1] // 2
    writes, reads = select_ref[:, :half], select_ref[:, half:]
    gate, scanned, d_update = gate_ref[...], scanned_ref[...], d_update_ref[...]
    sigmoid = 1.0 / (1.0 + jnp.exp(-gate))
    gated = scanned * (gate * sigmoid)
    d_gain_ref[...] += jnp.sum(d_update * gated, axis=0, keepdims=True)
    d_gated = d_update * gain_ref[...] - factor_ref[...] * gated
    d_gate = d_gated * scanned * (sigmoid * (1.0 + gate * (1.0 - sigmoid)))
    d_gate_ref[...] = d_gate.astype(jnp.bfloat16)
    grads = d_gated * (gate * sigmoid)
    grads_low = grads.astype(jnp.bfloat16)
    d_skip_ref[...] += jnp.sum(grads * wide, axis=0, keepdims=True)
    scores = mixed_dot(reads, writes, ((1,), (1,)))
    last = logs[GROUP - 1 : GROUP, :]
    fades = jnp.exp(last - logs)
    tails = fades * steps
    ends = jnp.exp(last)
    before, after = states_ref[0], carry[...]
    before_low, after_low = before.astype(jnp.bfloat16), after.astype(jnp.bfloat16)
    grown = jnp.exp(logs)
    scaled = grads * spread(grown, width)
    across = mixed_dot(reads, before_low) * scaled
    back = mixed_dot(writes, after_low)
    tails_wide = spread(tails, width)
    touched = wide * back
    d_reads = mixed_dot(scaled, before_low, ((1,), (1,)))
    d_writes = mixed_dot(wide * tails_wide, after_low, ((1,), (1,)))
    products = jnp.sum(before * after, axis=0, keepdims=True)
    carry[...] = after * spread(ends, width) + mixed_dot(reads, scaled, ((0,), (0,)))
    d_scores = jnp.zeros((GROUP, GROUP), jnp.float32)
    head_ids = lax.broadcasted_iota(jnp.int32, (1, heads), 1)
    row_ids = lax.broadcasted_iota(jnp.int32, (heads, 1), 0)
    row_sums = jnp.zeros((GROUP, heads), jnp.float32)
    d_tails = jnp.zeros((GROUP, heads), jnp.float32)
    d_ends = jnp.zeros((1, heads), jnp.float32)
    col_sums = jnp.zeros((heads, GROUP), jnp.float32)
    insides = []
    for h in range(heads):
        at = slice(h * width, (h + 1) * width)
        row = flat[h : h + 1, :]
        decays = jnp.exp(jnp.where(lower, logs[:, h : h + 1] - logs_flat[h : h + 1, :], -1e30))
        d_weights = mixed_dot(grads_low[:, at], x[:, at], ((1,), (1,)))
        kept = scores * decays
        insides.append(mixed_dot(kept * row, grads_low[:, at], ((0,), (0,))))
        d_scores = d_scores + d_weights * (decays * row)
        reach = d_weights * kept
        sums = jnp.sum(reach * row, axis=1, keepdims=True)
        sums = sums + jnp.sum(across[:, at], axis=1, keepdims=True)
        mine = head_ids == h
        row_sums = jnp.where(mine, sums, row_sums)
        col_sums = jnp.where(row_ids == h, jnp.sum(reach, axis=0, keepdims=True), col_sums)
        d_tails = jnp.where(mine, jnp.sum(touched[:, at], axis=1, keepdims=True), d_tails)
        d_ends = jnp.where(mine, jnp.sum(products[:, at], axis=1, keepdims=True), d_ends)
    corner = jnp.where(
        lax.broadcasted_iota(jnp.int32, (heads, heads), 0)
        == lax.broadcasted_iota(jnp.int32, (heads, heads), 1),
        1.0,
        0.0,
    ).astype(jnp.float32)
    reached = exact_dot(col_sums, corner, ((0,), (0,)))
    pulled = d_tails * tails
    d_last = d_ends * ends + jnp.sum(pulled, axis=0, keepdims=True)
    d_logs = row_sums - reached * steps - pulled
    d_rates = exact_dot(ones, d_logs, ((0,), (0,))) + d_last
    d_rate_ref[...] += jnp.sum(d_rates * steps, axis=0, keepdims=True)
    d_steps_ref[...] = d_rates * rate + reached + d_tails * fades
    d_x_ref[...] = (
        jnp.concatenate(insides, axis=1) + tails_wide * back + skip_ref[...] * grads
    )
    d_scores = d_scores.astype(jnp.bfloat16)
    d_select_ref[:, :half] = d_writes + mixed_dot(d_scores, reads, ((0,), (0,)))
    d_select_ref[:, half:] = d_reads + mixed_dot(d_scores, writes)


def kernel_specs(tokens, inner, heads, states, reverse):
    count = tokens // GROUP

    def at(i):
        return count - 1 - i if reverse else i

    def rows(cols):
        return pl.BlockSpec((GROUP, cols), lambda i: (at(i), 0))

    def fixed(height, cols):
        return pl.BlockSpec((height, cols), lambda i: (0, 0))

    shared = [
        rows(inner),
        rows(heads),
        pl.BlockSpec((heads, GROUP), lambda i: (0, at(i))),
        fixed(1, heads),
        fixed(heads, 1),
        rows(2 * states),
        fixed(1, inner),
        rows(inner),
        fixed(1, inner),
    ]
    kept = pl.BlockSpec((1, states, inner), lambda i: (at(i), 0, 0))
    return count, rows, fixed, shared, kept


def shape(dims, kind=jnp.float32):
    return jax.ShapeDtypeStruct(dims, kind)


def scan_forward(shared):
    tokens, inner = shared[0].shape
    heads, states = shared[1].shape[1], shared[5].shape[1] // 2
    count, rows, fixed, specs, kept = kernel_specs(SEQ_LEN, inner, heads, states, False)
    return pl.pallas_call(
        forward_kernel,
        grid=(count,),
        in_specs=specs,
        out_specs=[rows(inner), kept, rows(inner), rows(1)],
        out_shape=[
            shape((tokens, inner)),
            shape((count, states, inner)),
            shape((tokens, inner), jnp.bfloat16),
            shape((tokens, 1)),
        ],
        scratch_shapes=[pltpu.VMEM((states, inner), jnp.float32)],
    )(*shared)


def scan_backward(shared, scanned, kept_states, d_update, factor):
    tokens, inner = shared[0].shape
    heads, states = shared[1].shape[1], shared[5].shape[1] // 2
    count, rows, fixed, specs, kept = kernel_specs(SEQ_LEN, inner, heads, states, True)
    return pl.pallas_call(
        backward_kernel,
        grid=(count,),
        in_specs=specs + [rows(inner), kept, rows(inner), rows(1)],
        out_specs=[
            rows(inner), rows(2 * states), rows(heads), rows(inner),
            fixed(1, heads), fixed(1, inner), fixed(1, inner),
        ],
        out_shape=[
            shape((tokens, inner)), shape((tokens, 2 * states)), shape((tokens, heads)),
            shape((tokens, inner), jnp.bfloat16),
            shape((1, heads)), shape((1, inner)), shape((1, inner)),
        ],
        scratch_shapes=[pltpu.VMEM((states, inner), jnp.float32)],
    )(*shared, scanned, kept_states, d_update, factor)


def swap(values, bit):
    count = lax.axis_size("tensor")
    return lax.ppermute(values, "tensor", [(i, i ^ bit) for i in range(count)])


def tensor_sum_small(values):
    bit = 1
    while bit < lax.axis_size("tensor"):
        values = values + swap(values, bit)
        bit *= 2
    return values


def halves(values, bit):
    half = values.shape[0] // 2
    upper = (lax.axis_index("tensor") & bit) // bit
    mine = lax.dynamic_slice_in_dim(values, upper * half, half)
    other = lax.dynamic_slice_in_dim(values, (1 - upper) * half, half)
    return mine, other


def joined(mine, other, bit):
    upper = (lax.axis_index("tensor") & bit) // bit
    half = mine.shape[0]
    whole = jnp.zeros((2 * half,) + mine.shape[1:], mine.dtype)
    whole = lax.dynamic_update_slice_in_dim(whole, mine, upper * half, 0)
    return lax.dynamic_update_slice_in_dim(whole, other, (1 - upper) * half, 0)


def tensor_scatter(values):
    bit = 1
    while bit < lax.axis_size("tensor"):
        mine, other = halves(values, bit)
        values = mine + swap(other, bit)
        bit *= 2
    return values


def tensor_gather(values):
    bit = lax.axis_size("tensor") // 2
    while bit:
        values = joined(values, swap(values, bit), bit)
        bit //= 2
    return values


def tensor_sum(values):
    mine, other = halves(values, 1)
    mine = mine + swap(other, 1)
    bit = 2
    while bit < lax.axis_size("tensor"):
        mine = mine + swap(mine, bit)
        bit *= 2
    return joined(mine, swap(mine, 1), 1)


def ring_fits():
    n = lax.axis_size("dp")
    return n <= 8 and n % 2 == 0


def ring_sum(values):
    n = lax.axis_size("dp")
    if not ring_fits():
        return lax.psum(values, "dp")
    order = list(range(0, n, 2)) + list(range(n - 1, 0, -2))
    places = [0] * n
    for place, device in enumerate(order):
        places[device] = place
    me = jnp.array(places, jnp.int32)[lax.axis_index("dp")]
    ahead = [(order[i], order[(i + 1) % n]) for i in range(n)]
    behind = [(b, a) for a, b in ahead]

    def start(place, side):
        return 2 * ((place + 2 * n) % n) + side

    def take(place, side):
        return lax.dynamic_slice_in_dim(values, start(place, side), 1)

    front, back = take(me, 0), take(me, 1)
    for step in range(1, n):
        front = lax.ppermute(front, "dp", ahead) + take(me - step, 0)
        back = lax.ppermute(back, "dp", behind) + take(me + step, 1)
    whole = values
    for step in range(n):
        whole = lax.dynamic_update_slice(whole, front, (start(me + 1 - step, 0), 0, 0))
        whole = lax.dynamic_update_slice(whole, back, (start(me - 1 + step, 1), 0, 0))
        if step < n - 1:
            front = lax.ppermute(front, "dp", ahead)
            back = lax.ppermute(back, "dp", behind)
    return whole


def packed(parts, multiple):
    flat = jnp.concatenate([part.reshape(-1) for part in parts])
    return jnp.pad(flat, (0, -flat.shape[0] % multiple))


def unpacked(flat, parts):
    results, at = [], 0
    for part in parts:
        results.append(flat[at : at + part.size].reshape(part.shape))
        at += part.size
    return results


def body(
    hidden,
    cotangent,
    norm_gain,
    gate_weight,
    value_weight,
    step_weight,
    state_weight,
    value_kernel,
    value_offset,
    state_kernel,
    state_offset,
    step_offset,
    log_decay,
    skip_gain,
    mixer_gain,
    output_weight,
):
    source = hidden.astype(jnp.float32)
    recip = lax.rsqrt(jnp.mean(source * source, axis=1, keepdims=True) + epsilon)
    scaled = source * recip
    normed = (scaled * norm_gain).astype(jnp.bfloat16)
    gate_raw = plain(normed, gate_weight)
    value_raw = plain(normed, value_weight)
    step_raw = plain(normed, step_weight)
    select_raw = plain(normed, state_weight)
    (conv_values, conv_selects), conv_back = jax.vjp(
        both_convs, value_raw, select_raw, value_kernel, value_offset, state_kernel, state_offset
    )
    inputs = conv_values.astype(jnp.bfloat16)
    selects = conv_selects.astype(jnp.bfloat16)
    step_total = step_raw + step_offset
    timing = jax.nn.softplus(step_total)
    decay_rate = -jnp.exp(log_decay)
    heads = timing.shape[1]
    width = inputs.shape[1] // heads
    shared_inputs = (
        inputs, timing, timing.T, decay_rate[None, :], decay_rate[:, None], selects,
        jnp.repeat(skip_gain, width)[None, :], gate_raw, mixer_gain[None, :],
    )
    scanned, kept_states, update, local_squares = scan_forward(shared_inputs)
    branch_part = plain(update, output_weight)
    upstream = cotangent.astype(jnp.float32)
    local_dots = jnp.sum(upstream * branch_part, axis=1)
    squares, d_scale = tensor_sum_small(jnp.stack([local_squares[:, 0], local_dots]))
    d_scale = d_scale[:, None]
    projected = tensor_sum(branch_part)
    scale = lax.rsqrt(squares / INNER + epsilon)[:, None]
    output = (source + projected * scale).astype(jnp.bfloat16)
    d_projected = (upstream * scale).astype(jnp.bfloat16)
    output_grad = weight_product(update, d_projected)
    d_update = back_product(d_projected, output_weight)
    factor = d_scale * scale**3 / INNER
    d_inputs, d_selects, d_timing, gate_low, d_rate, d_skip, d_gain = scan_backward(
        shared_inputs, scanned, kept_states, d_update, factor
    )
    d_step = d_timing * jax.nn.sigmoid(step_total)
    timing_grad = jnp.sum(d_step, axis=0)
    decay_grad = d_rate[0] * decay_rate
    skip_grad = jnp.sum(d_skip.reshape(heads, width), axis=1)
    mixing_grad = d_gain[0]
    d_value, d_select, kernel_grad, offset_grad, filter_part, shift_part = conv_back(
        (d_inputs, d_selects)
    )
    value_low = d_value.astype(jnp.bfloat16)
    step_low = d_step.astype(jnp.bfloat16)
    select_low = d_select.astype(jnp.bfloat16)
    normed_part = back_product(gate_low, gate_weight) + back_product(value_low, value_weight)
    normed_part = (
        normed_part + back_product(step_low, step_weight) + back_product(select_low, state_weight)
    )
    d_normed = tensor_sum(normed_part)
    both_grad = weight_product(normed, jnp.concatenate([gate_low, value_low], axis=1))
    step_grad = weight_product(normed, step_low)
    state_part = weight_product(normed, select_low)
    gain_grad = jnp.sum(normed_part * scaled, axis=0)
    d_scaled = d_normed * norm_gain
    d_recip = jnp.sum(d_scaled * source, axis=1, keepdims=True)
    hidden_grad = upstream + d_scaled * recip - d_recip * recip**3 * source / D
    output_grad = lax.psum(output_grad, "dp")
    shared = [state_part, gain_grad, filter_part, shift_part]
    own = [step_grad, kernel_grad, offset_grad, timing_grad, decay_grad, skip_grad, mixing_grad]
    lane = 128
    shares = lax.axis_size("tensor")
    quarter = tensor_scatter(packed(shared, 8 * lane * shares).reshape(-1, lane))
    pieces = 2 * lax.axis_size("dp") if ring_fits() else 2
    wide = both_grad.shape[1]
    small = packed([quarter] + own, pieces * 8 * wide).reshape(pieces, -1, wide)
    large = both_grad.reshape(pieces, -1, wide)
    tall = large.shape[1]
    summed = ring_sum(jnp.concatenate([large, small], axis=1))
    gate_grad, value_grad = jnp.split(summed[:, :tall].reshape(both_grad.shape), 2, axis=1)
    quarter, *own = unpacked(summed[:, tall:].reshape(-1), [quarter] + own)
    step_grad, kernel_grad, offset_grad, timing_grad, decay_grad, skip_grad, mixing_grad = own
    state_grad, gain_grad, filter_grad, shift_grad = unpacked(tensor_gather(quarter).reshape(-1), shared)
    return (
        output,
        hidden_grad,
        gain_grad,
        gate_grad,
        value_grad,
        step_grad,
        state_grad,
        kernel_grad,
        offset_grad,
        filter_grad,
        shift_grad,
        timing_grad,
        decay_grad,
        skip_grad,
        mixing_grad,
        output_grad,
    )


def solution(mesh):
    return jax.shard_map(
        body,
        mesh=mesh,
        in_specs=(
            P("dp", None),
            P("dp", None),
            P(),
            P(None, "tensor"),
            P(None, "tensor"),
            P(None, "tensor"),
            P(),
            P(None, "tensor"),
            P("tensor"),
            P(),
            P(),
            P("tensor"),
            P("tensor"),
            P("tensor"),
            P("tensor"),
            P("tensor", None),
        ),
        out_specs=(
            P("dp", None),
            P("dp", None),
            P(),
            P(None, "tensor"),
            P(None, "tensor"),
            P(None, "tensor"),
            P(),
            P(None, "tensor"),
            P("tensor"),
            P(),
            P(),
            P("tensor"),
            P("tensor"),
            P("tensor"),
            P("tensor"),
            P("tensor", None),
        ),
        check_vma=False,
    )
```
